32 devices in a mesh: seq: 4 (over x, core), chan: 8 (over z, y).
Axes of the slice: x: 2, y: 2, z: 4, core: 2. Of those that a mesh axis runs over, the one named last changes fastest.
Arguments:
- d_out: bfloat16 [2048, 8192], P('seq', 'chan'), may hold values from -6 to 6
- w_out: bfloat16 [1024, 8192], P('chan'), may hold values from -0.0625 to 0.0625
- gate: bfloat16 [2048, 1024], P('seq', 'chan'), may hold values from -6 to 6
- inner: bfloat16 [2048, 1024], P('seq', 'chan'), may hold values from -0.125 to 0.125
- filt: bfloat16 [2048, 1024], P('seq', 'chan'), may hold values from -4 to 4
Outputs:
- grad_inner: bfloat16 [2048, 1024], P('seq', 'chan')
- grad_filter: float32 [2048, 1024], P('seq', 'chan')
The draws below stay inside these ranges and needn't reach their ends.
All inputs are finite; a program needn't handle non-finite values.
Results may differ from the reference program's by a relative error of at most 0.005.
Values may be sent and summed in bfloat16 or wider, within the bound.
No kernel may reach another device: no remote copies, remote signals or barrier semaphores. Data moves between devices by JAX's collectives and lax.ppermute only.
A program may use at most 64 MiB of HBM per device.

```python
import jax
import jax.numpy as jnp
from jax import lax

D = 8192
C_DEV = 128
CHANNELS = 1024
LENGTH = 2048


def draw_filt(key, part):
    keys = jax.random.split(key, 4)
    lag_ids = jnp.arange(LENGTH, dtype=jnp.int32)[:, None]
    lags = lag_ids.astype(jnp.float32)
    log_rate = jax.random.uniform(keys[0], (CHANNELS,), jnp.float32, jnp.log(0.5 / LENGTH), jnp.log(1.0 / 30.0))
    noise = jax.random.truncated_normal(keys[1], -4.0, 4.0, (LENGTH, CHANNELS), jnp.float32)
    rate = jnp.exp(log_rate)
    places = jax.random.randint(keys[2], (4, CHANNELS), 0, LENGTH)
    drops = jax.random.uniform(keys[3], (4, CHANNELS), jnp.float32, 0.5, 0.8)
    envelope = jnp.exp(-rate[None, :] * lags)
    for which in range(4):
        envelope = envelope * jnp.where(lag_ids >= places[which][None, :], drops[which][None, :], 1.0)
    scale = jnp.sqrt(1.0 - jnp.exp(-2.0 * rate))
    return (noise * scale[None, :] * envelope).astype(jnp.bfloat16)


def steps_of(stream_key, dims, pieces, least, high):
    def one(axis_at, parts):
        heights = jax.random.uniform(jax.random.fold_in(jax.random.fold_in(stream_key, 6), axis_at), (parts,), jnp.float32, least / len(pieces), high / len(pieces))
        return jnp.repeat(jnp.exp(heights), dims[axis_at] // parts).reshape((-1,) + (1,) * (len(dims) - axis_at - 1))

    level = one(*pieces[0])
    for cut in pieces[1:]:
        level = level * one(*cut)
    return level


def bell_draw(key, extent, width, most, cuts=(), kind=jnp.bfloat16):
    loudness = steps_of(key, extent, cuts, -0.22, 0.18) if cuts else 1.0
    drawn = jax.random.normal(key, extent, jnp.float32) * width * loudness
    return jnp.minimum(jnp.maximum(drawn, -most), most).astype(kind)


def setup_inputs(seed: int = 0) -> dict:
    key_list = jax.random.split(jax.random.key(seed), 6)
    return {
        "d_out": bell_draw(key_list[0], (LENGTH, D), 1.0, 6.0, ((0, 4), (1, 8))),
        "w_out": bell_draw(key_list[1], (CHANNELS, D), D ** -0.5, 0.0625, ((0, 8),)),
        "gate": bell_draw(key_list[2], (LENGTH, CHANNELS), 1.0, 6.0, ((0, 4), (1, 8))),
        "inner": bell_draw(key_list[3], (LENGTH, CHANNELS), LENGTH ** -0.5, 0.125, ((0, 4), (1, 8))),
        "filt": draw_filt(jax.random.fold_in(key_list[5], 71), 0),
    }


def correlate(first, second):
    rows = first.shape[0]
    size = 2 * rows
    spec_a = jnp.fft.rfft(first, n=size, axis=0)
    spec_b = jnp.fft.rfft(second, n=size, axis=0)
    return jnp.fft.irfft(jnp.conj(spec_a) * spec_b, n=size, axis=0)[:rows]


def reference(d_out, w_out, gate, inner, filt):
    grad_gated = jnp.dot(d_out, w_out.T, preferred_element_type=jnp.float32)
    grad_conv = (gate.astype(jnp.float32) * grad_gated).astype(jnp.bfloat16)
    groups = CHANNELS // C_DEV

    def split_groups(values):
        return jnp.moveaxis(values.astype(jnp.float32).reshape(LENGTH, groups, C_DEV), 1, 0)

    def one_group(items):
        conv_part, filt_part, inner_part = items
        return correlate(filt_part, conv_part), correlate(inner_part, conv_part)

    grad_i, grad_f = lax.map(one_group, (split_groups(grad_conv), split_groups(filt), split_groups(inner)))

    def join_groups(values):
        return jnp.moveaxis(values, 0, 1).reshape(LENGTH, CHANNELS)

    return join_groups(grad_i).astype(jnp.bfloat16), join_groups(grad_f).astype(jnp.float32)
```

```python
import functools
import math

import jax
import jax.numpy as jnp
import numpy as np
from jax import lax
from jax.experimental import pallas as pl
from jax.experimental.pallas import tpu as pltpu
from jax.sharding import PartitionSpec as P

SUB = 256
VMEM = pl.BlockSpec(memory_space=pltpu.VMEM)
SMEM = pl.BlockSpec(memory_space=pltpu.SMEM)
F32, BF16 = jnp.float32, jnp.bfloat16
NT = (((1,), (1,)), ((), ()))


def swapped(block, axis, mask):
    size = lax.axis_size(axis)
    return lax.ppermute(block, axis, [(i, i ^ mask) for i in range(size)])


def dft_parts():
    freq = np.arange(SUB)[:, None]
    place = np.arange(SUB)[None, :]
    angle = (((2 * freq + 1) * place) % (4 * SUB)).astype(np.float64) * (math.pi / (2 * SUB))
    matrix = np.concatenate([np.cos(angle), -np.sin(angle)], axis=0).astype(np.float32)
    upper = matrix.astype(jnp.bfloat16)
    lower = (matrix - upper.astype(np.float32)).astype(jnp.bfloat16)
    return upper, lower


def dot(a, b):
    return jnp.dot(a, b, preferred_element_type=F32)


def product_kernel(count, out_type, core_ref, d_ref, *refs):
    mine, other, out_ref = refs[:count], refs[count : 2 * count], refs[2 * count]
    half = d_ref.shape[1] // 2
    core = core_ref[0]
    d_mine = d_ref[:, pl.ds(pl.multiple_of(core * half, half), half)]
    d_other = d_ref[:, pl.ds(pl.multiple_of((1 - core) * half, half), half)]
    for i in range(count):
        total = lax.dot_general(d_mine, mine[i][...], NT, preferred_element_type=F32)
        total += lax.dot_general(d_other, other[i][...], NT, preferred_element_type=F32)
        out_ref[i] = total.astype(out_type)


def product(core, d_out, mine, other, out_type):
    count = len(mine)
    rows, channels = d_out.shape[0], mine[0].shape[0]
    return pl.pallas_call(
        functools.partial(product_kernel, count, out_type),
        out_shape=jax.ShapeDtypeStruct((count, rows, channels), out_type),
        in_specs=[SMEM] + [VMEM] * (1 + 2 * count),
        out_specs=VMEM,
        cost_estimate=pl.CostEstimate(
            flops=2 * count * rows * channels * d_out.shape[1], bytes_accessed=4 << 20, transcendentals=0
        ),
    )(core, d_out, *mine, *other)


def lag_kernel(n, seq_ref, up_ref, low_ref, *refs):
    blocks, out_ref, spec = refs[:n], refs[n], refs[n + 1]
    me = seq_ref[0]
    spec[0] = jnp.zeros_like(spec[0])
    for offset in range(n):
        place = (me ^ offset) * 2 + 1
        for sub in range(2):
            rows = pl.ds(sub * SUB, SUB)
            data = jnp.concatenate([blocks[offset][0, rows, :], blocks[offset][1, rows, :]], axis=1)
            both = dot(up_ref[...], data) + dot(low_ref[...], data)
            channels = data.shape[1] // 2
            spec[place + sub, 0] = both[:, :channels] * (1.0 / SUB)
            spec[place + sub, 1] = both[:, channels:] * (1.0 / SUB)
    channels = spec.shape[-1]
    sign = (1 - 2 * (lax.broadcasted_iota(jnp.int32, (SUB, channels), 0) % 2)).astype(F32)

    @pl.loop(0, 2 * n)
    def _(lag):
        for which in range(2):
            out_ref[lag, which, :SUB] = spec[lag + 1, which, :SUB] - sign * spec[lag, which, SUB:]
            out_ref[lag, which, SUB:] = spec[lag + 1, which, SUB:] + sign * spec[lag, which, :SUB]


def lag_spectra(seq_id, upper, lower, blocks):
    n = len(blocks)
    channels = blocks[0].shape[-1]
    return pl.pallas_call(
        functools.partial(lag_kernel, n),
        out_shape=jax.ShapeDtypeStruct((2 * n, 2, 2 * SUB, channels), F32),
        in_specs=[SMEM] + [VMEM] * (2 + n),
        out_specs=VMEM,
        scratch_shapes=[pltpu.VMEM((2 * n + 1, 2, 2 * SUB, channels), F32)],
        cost_estimate=pl.CostEstimate(
            flops=16 * n * SUB * SUB * channels * 2, bytes_accessed=6 << 20, transcendentals=0
        ),
    )(seq_id, upper, lower, *blocks)


CHUNK = 32


def conv_kernel(n, seq_ref, up_ref, low_ref, upt_ref, lowt_ref, lag_ref, *refs):
    blocks = refs[:n]
    inner_ref, filter_ref, spec, total = refs[n:]
    me = seq_ref[0]
    channels = spec.shape[-1]
    for offset in range(n):
        block = me ^ offset

        @pl.when(block >= me)
        def _():
            data = jnp.concatenate([blocks[offset][:SUB, :], blocks[offset][SUB:, :]], axis=1)
            both = dot(up_ref[...], data) + dot(low_ref[...], data)
            place = (block - me) * 2
            spec[place] = both[:, :channels]
            spec[place + 1] = both[:, channels:]

    steps = (n - me) * 2
    for chunk in range(SUB // CHUNK):
        real, imag = pl.ds(chunk * CHUNK, CHUNK), pl.ds(SUB + chunk * CHUNK, CHUNK)

        def advance(step, carry):
            sums, earlier = carry
            g_real, g_imag = spec[step, real, :], spec[step, imag, :]
            now = tuple((lag_ref[step, which, real, :], lag_ref[step, which, imag, :]) for which in range(2))
            out = []
            for which in range(2):
                for k_real, k_imag in (now[which], earlier[which]):
                    s_real, s_imag = sums[len(out)]
                    s_real = s_real + g_real * k_real + g_imag * k_imag
                    s_imag = s_imag + g_imag * k_real - g_real * k_imag
                    out.append((s_real, s_imag))
            return tuple(out), now

        zero = jnp.zeros((CHUNK, channels), F32)
        start = (((zero, zero),) * 4, ((zero, zero),) * 2)
        sums, _ = lax.fori_loop(0, steps, advance, start)
        for i in range(4):
            total[real, i * channels : (i + 1) * channels] = sums[i][0]
            total[imag, i * channels : (i + 1) * channels] = sums[i][1]
    for which in range(2):
        whole = total[:, 2 * which * channels : 2 * (which + 1) * channels]
        high = whole.astype(BF16)
        low = (whole - high.astype(F32)).astype(BF16)
        values = dot(upt_ref[...], high) + (dot(lowt_ref[...], high) + dot(upt_ref[...], low))
        out_ref = (inner_ref, filter_ref)[which]
        out_ref[:SUB, :] = values[:, :channels].astype(out_ref.dtype)
        out_ref[SUB:, :] = values[:, channels:].astype(out_ref.dtype)


def convolve(seq_id, parts, parts_t, lags, blocks):
    n = len(blocks)
    rows, channels = blocks[0].shape
    return pl.pallas_call(
        functools.partial(conv_kernel, n),
        out_shape=(
            jax.ShapeDtypeStruct((rows, channels), BF16),
            jax.ShapeDtypeStruct((rows, channels), F32),
        ),
        in_specs=[SMEM] + [VMEM] * (5 + n),
        out_specs=(VMEM, VMEM),
        scratch_shapes=[
            pltpu.VMEM((2 * n, 2 * SUB, channels), F32),
            pltpu.VMEM((2 * SUB, 4 * channels), F32),
        ],
        cost_estimate=pl.CostEstimate(
            flops=16 * n * SUB * SUB * channels * 2, bytes_accessed=8 << 20, transcendentals=0
        ),
    )(seq_id, *parts, *parts_t, lags, *blocks)


def spread_blocks(block, axis):
    size = lax.axis_size(axis)
    held = {0: block}
    mask = size // 2
    while mask:
        for offset in list(held):
            held[offset | mask] = swapped(held[offset], axis, mask)
        mask //= 2
    return [held[i] for i in range(size)]


def body(d_out, w_out, gate, inner, filt):
    seq_n, chan_n = lax.axis_size("seq"), lax.axis_size("chan")
    seq, chan = lax.axis_index("seq"), lax.axis_index("chan")
    core = seq % 2
    seq_id, core_id = seq.astype(jnp.int32)[None], core.astype(jnp.int32)[None]
    features = d_out.shape[1]
    half = features // 2

    def piece(mask, which):
        start = (chan ^ mask) * features + which * half
        return lax.dynamic_slice(w_out, (0, start), (w_out.shape[0], half))

    fetched, other = {}, {}
    order = [m for m in range(chan_n) if m % 2] + [m for m in range(1, chan_n) if m % 2 == 0]
    for mask in order:
        fetched[mask] = swapped(piece(mask, core), "chan", mask)
    for mask in order:
        other[mask] = swapped(fetched[mask], "seq", 1)
    fetched[0], other[0] = piece(0, core), piece(0, 1 - core)
    odd = [m for m in range(chan_n) if m % 2]
    even = [m for m in range(chan_n) if m % 2 == 0]
    p_odd = product(core_id, d_out, [fetched[m] for m in odd], [other[m] for m in odd], BF16)
    from_pair = swapped(p_odd, "chan", 1)
    p_even = product(core_id, d_out, [fetched[m] for m in even], [other[m] for m in even], F32)
    sums = [p_even[i] + from_pair[i].astype(F32) for i in range(chan_n // 2)]
    grad_gated = sums[0]
    arrived = [swapped(sums[i].astype(BF16), "chan", 2 * i) for i in range(1, chan_n // 2)]
    for block in arrived:
        grad_gated = grad_gated + block.astype(F32)
    grad_conv = (gate.astype(F32) * grad_gated).astype(BF16)

    upper, lower = dft_parts()
    lag_blocks = spread_blocks(jnp.stack([filt, inner]), "seq")
    lags = lag_spectra(seq_id, upper, lower, lag_blocks)
    grad_blocks = spread_blocks(grad_conv, "seq")
    return tuple(convolve(seq_id, (upper, lower), (upper.T, lower.T), lags, grad_blocks))


def solution(mesh):
    placed = (
        P("seq", "chan"),
        P("chan", None),
        P("seq", "chan"),
        P("seq", "chan"),
        P("seq", "chan"),
    )
    return jax.shard_map(
        body,
        mesh=mesh,
        in_specs=placed,
        out_specs=(P("seq", "chan"), P("seq", "chan")),
        check_vma=False,
    )
```

```python
import functools
import math

import jax
import jax.numpy as jnp
import numpy as np
from jax import lax
from jax.experimental import pallas as pl
from jax.experimental.pallas import tpu as pltpu
from jax.sharding import PartitionSpec as P

SUB = 256
VMEM = pl.BlockSpec(memory_space=pltpu.VMEM)
SMEM = pl.BlockSpec(memory_space=pltpu.SMEM)
F32, BF16 = jnp.float32, jnp.bfloat16
NT = (((1,), (1,)), ((), ()))


def swapped(block, axis, mask):
    size = lax.axis_size(axis)
    return lax.ppermute(block, axis, [(i, i ^ mask) for i in range(size)])


def dft_parts():
    freq = np.arange(SUB)[:, None]
    place = np.arange(SUB)[None, :]
    angle = (((2 * freq + 1) * place) % (4 * SUB)).astype(np.float64) * (math.pi / (2 * SUB))
    matrix = np.concatenate([np.cos(angle), -np.sin(angle)], axis=0).astype(np.float32)
    upper = matrix.astype(jnp.bfloat16)
    lower = (matrix - upper.astype(np.float32)).astype(jnp.bfloat16)
    return upper, lower


def dot(a, b):
    return jnp.dot(a, b, preferred_element_type=F32)


def product_kernel(count, rows, out_type, core_ref, d_ref, *refs):
    mine, other, out_ref = refs[:count], refs[count : 2 * count], refs[2 * count]
    half = d_ref.shape[1] // 2
    core = core_ref[0]
    d_mine = d_ref[rows, pl.ds(pl.multiple_of(core * half, half), half)]
    d_other = d_ref[rows, pl.ds(pl.multiple_of((1 - core) * half, half), half)]
    channels = mine[0].shape[0]
    for i in range(0, count, 2):
        w_mine = jnp.concatenate([mine[i][...], mine[i + 1][...]], axis=0)
        w_other = jnp.concatenate([other[i][...], other[i + 1][...]], axis=0)
        total = lax.dot_general(d_mine, w_mine, NT, preferred_element_type=F32)
        total += lax.dot_general(d_other, w_other, NT, preferred_element_type=F32)
        out_ref[i] = total[:, :channels].astype(out_type)
        out_ref[i + 1] = total[:, channels:].astype(out_type)


def product(core, d_out, mine, other, which, out_type):
    count = len(mine)
    channels = mine[0].shape[0]
    return pl.pallas_call(
        functools.partial(product_kernel, count, pl.ds(which * SUB, SUB), out_type),
        out_shape=jax.ShapeDtypeStruct((count, SUB, channels), out_type),
        in_specs=[SMEM] + [VMEM] * (1 + 2 * count),
        out_specs=VMEM,
        compiler_params=pltpu.CompilerParams(vmem_limit_bytes=8 << 20),
        cost_estimate=pl.CostEstimate(
            flops=2 * count * SUB * channels * d_out.shape[1], bytes_accessed=2 << 20, transcendentals=0
        ),
    )(core, d_out, *mine, *other)


def lag_kernel(n, seq_ref, up_ref, low_ref, *refs):
    blocks, out_ref, spec = refs[:n], refs[n], refs[n + 1]
    me = seq_ref[0]
    spec[0] = jnp.zeros_like(spec[0])
    out_ref[0] = jnp.zeros_like(out_ref[0])
    for offset in range(n):
        place = (me ^ offset) * 2 + 1
        for sub in range(2):
            rows = pl.ds(sub * SUB, SUB)
            data = jnp.concatenate([blocks[offset][0, rows, :], blocks[offset][1, rows, :]], axis=1)
            both = dot(up_ref[...], data) + dot(low_ref[...], data)
            channels = data.shape[1] // 2
            spec[place + sub, 0] = both[:, :channels] * (1.0 / SUB)
            spec[place + sub, 1] = both[:, channels:] * (1.0 / SUB)
    channels = spec.shape[-1]
    sign = (1 - 2 * (lax.broadcasted_iota(jnp.int32, (SUB, channels), 0) % 2)).astype(F32)

    @pl.loop(0, 2 * n)
    def _(lag):
        for which in range(2):
            out_ref[lag + 1, which, :SUB] = spec[lag + 1, which, :SUB] - sign * spec[lag, which, SUB:]
            out_ref[lag + 1, which, SUB:] = spec[lag + 1, which, SUB:] + sign * spec[lag, which, :SUB]


def lag_spectra(seq_id, upper, lower, blocks):
    n = len(blocks)
    channels = blocks[0].shape[-1]
    return pl.pallas_call(
        functools.partial(lag_kernel, n),
        out_shape=jax.ShapeDtypeStruct((2 * n + 1, 2, 2 * SUB, channels), F32),
        in_specs=[SMEM] + [VMEM] * (2 + n),
        out_specs=VMEM,
        scratch_shapes=[pltpu.VMEM((2 * n + 1, 2, 2 * SUB, channels), F32)],
        compiler_params=pltpu.CompilerParams(vmem_limit_bytes=(4 + 3 * n) << 20),
        cost_estimate=pl.CostEstimate(
            flops=16 * n * SUB * SUB * channels * 2, bytes_accessed=6 << 20, transcendentals=0
        ),
    )(seq_id, upper, lower, *blocks)


CHUNK = 32


def add_kernel(n, which, last, seq_ref, up_ref, low_ref, lag_ref, *refs):
    blocks, refs = refs[:n], refs[n:]
    if last:
        before, upt_ref, lowt_ref, inner_ref, filter_ref, spec, total = refs
    else:
        total, spec = refs
    me = seq_ref[0]
    channels = spec.shape[-1]
    for pair in range(n // 2):
        offsets = (2 * pair, 2 * pair + 1)

        @pl.when(jnp.maximum(me ^ offsets[0], me ^ offsets[1]) >= me)
        def _():
            data = jnp.concatenate([blocks[o][...] for o in offsets], axis=1)
            both = dot(up_ref[...], data) + dot(low_ref[...], data)
            for i in range(2):
                spec[me ^ offsets[i]] = both[:, i * channels : (i + 1) * channels]

    for chunk in range(SUB // CHUNK):
        real, imag = pl.ds(chunk * CHUNK, CHUNK), pl.ds(SUB + chunk * CHUNK, CHUNK)

        def advance(step, sums):
            g_real, g_imag = spec[me + step, real, :], spec[me + step, imag, :]
            out = []
            for array in range(2):
                for sub in range(2):
                    lag = step * 2 + which - sub + 1
                    k_real, k_imag = lag_ref[lag, array, real, :], lag_ref[lag, array, imag, :]
                    s_real, s_imag = sums[len(out)]
                    s_real = s_real + g_real * k_real + g_imag * k_imag
                    s_imag = s_imag + g_imag * k_real - g_real * k_imag
                    out.append((s_real, s_imag))
            return tuple(out)

        if last:
            start = tuple(
                (before[real, i * channels : (i + 1) * channels], before[imag, i * channels : (i + 1) * channels])
                for i in range(4)
            )
        else:
            start = ((jnp.zeros((CHUNK, channels), F32),) * 2,) * 4
        sums = lax.fori_loop(0, n - me, advance, start)
        for i in range(4):
            total[real, i * channels : (i + 1) * channels] = sums[i][0]
            total[imag, i * channels : (i + 1) * channels] = sums[i][1]
    if not last:
        return
    for array in range(2):
        whole = total[:, 2 * array * channels : 2 * (array + 1) * channels]
        high = whole.astype(BF16)
        low = (whole - high.astype(F32)).astype(BF16)
        values = dot(upt_ref[...], high) + (dot(lowt_ref[...], high) + dot(upt_ref[...], low))
        out_ref = (inner_ref, filter_ref)[array]
        out_ref[:SUB, :] = values[:, :channels].astype(out_ref.dtype)
        out_ref[SUB:, :] = values[:, channels:].astype(out_ref.dtype)


def add_blocks(seq_id, parts, lags, blocks, which, before=None, parts_t=None):
    n = len(blocks)
    channels = blocks[0].shape[-1]
    last = before is not None
    whole = jax.ShapeDtypeStruct((2 * SUB, 4 * channels), F32)
    out_shape = whole
    scratch = [pltpu.VMEM((n, 2 * SUB, channels), F32)]
    if last:
        out_shape = (
            jax.ShapeDtypeStruct((2 * SUB, channels), BF16),
            jax.ShapeDtypeStruct((2 * SUB, channels), F32),
        )
        scratch.append(pltpu.VMEM(whole.shape, F32))
    args = (seq_id, *parts, lags, *blocks) + ((before, *parts_t) if last else ())
    return pl.pallas_call(
        functools.partial(add_kernel, n, which, last),
        out_shape=out_shape,
        in_specs=[SMEM] + [VMEM] * (len(args) - 1),
        out_specs=(VMEM, VMEM) if last else VMEM,
        scratch_shapes=scratch,
        compiler_params=pltpu.CompilerParams(vmem_limit_bytes=(6 + 2 * n) << 20),
        cost_estimate=pl.CostEstimate(
            flops=8 * n * SUB * SUB * channels * 2, bytes_accessed=4 << 20, transcendentals=0
        ),
    )(*args)


def spread_blocks(block, axis):
    size = lax.axis_size(axis)
    held = {0: block}
    mask = size // 2
    while mask:
        for offset in list(held):
            held[offset | mask] = swapped(held[offset], axis, mask)
        mask //= 2
    return [held[i] for i in range(size)]


def body(d_out, w_out, gate, inner, filt):
    seq_n, chan_n = lax.axis_size("seq"), lax.axis_size("chan")
    seq, chan = lax.axis_index("seq"), lax.axis_index("chan")
    core = seq % 2
    seq_id, core_id = seq.astype(jnp.int32)[None], core.astype(jnp.int32)[None]
    features = d_out.shape[1]
    half = features // 2

    def piece(source, mask, which):
        start = (chan ^ mask) * features + which * half
        return lax.dynamic_slice(source, (0, start), (source.shape[0], half))

    odd = [m for m in reversed(range(chan_n)) if m % 2]
    even = [m for m in reversed(range(chan_n)) if m % 2 == 0]
    fetched, other = {}, {}
    for mask in odd:
        fetched[mask] = swapped(piece(w_out, mask, core), "chan", mask)
    w_later, fetched[odd[0]] = lax.optimization_barrier((w_out, fetched[odd[0]]))
    for mask in even[:-1]:
        fetched[mask] = swapped(piece(w_later, mask, core), "chan", mask)
    lag_blocks = spread_blocks(jnp.stack([filt, inner]), "seq")
    for mask in odd + even[:-1]:
        other[mask] = swapped(fetched[mask], "seq", 1)
    fetched[0], other[0] = piece(w_later, 0, core), piece(w_later, 0, 1 - core)
    upper, lower = dft_parts()

    def terms(masks, which, source, out_type):
        return product(core_id, source, [fetched[m] for m in masks], [other[m] for m in masks], which, out_type)

    p_odd = [terms(odd, which, d_out, BF16) for which in range(2)]
    from_pair = [swapped(p, "chan", 1) for p in p_odd]
    lags = lag_spectra(seq_id, upper, lower, lag_blocks)
    d_later, lags = lax.optimization_barrier((d_out, lags))
    p_even = [terms(even, which, d_later, F32) for which in range(2)]
    groups = chan_n // 2
    grad_blocks = []
    for which in range(2):
        sums = [p_even[which][i] + from_pair[which][i].astype(F32) for i in range(groups)]
        grad_gated = sums[-1]
        for i in range(groups - 1):
            grad_gated = grad_gated + swapped(sums[i].astype(BF16), "chan", even[i]).astype(F32)
        gate_part = gate[which * SUB : (which + 1) * SUB].astype(F32)
        grad_conv = (gate_part * grad_gated).astype(BF16)
        grad_blocks.append(spread_blocks(grad_conv, "seq"))
    first = add_blocks(seq_id, (upper, lower), lags, grad_blocks[0], 0)
    return tuple(add_blocks(seq_id, (upper, lower), lags, grad_blocks[1], 1, first, (upper.T, lower.T)))


def solution(mesh):
    placed = (
        P("seq", "chan"),
        P("chan", None),
        P("seq", "chan"),
        P("seq", "chan"),
        P("seq", "chan"),
    )
    return jax.shard_map(
        body,
        mesh=mesh,
        in_specs=placed,
        out_specs=(P("seq", "chan"), P("seq", "chan")),
        check_vma=False,
    )
```

```python
import functools
import math

import jax
import jax.numpy as jnp
import numpy as np
from jax import lax
from jax.experimental import pallas as pl
from jax.experimental.pallas import tpu as pltpu
from jax.sharding import PartitionSpec as P


SUB = 256
LANES = 128
VMEM = pl.BlockSpec(memory_space=pltpu.VMEM)
SMEM = pl.BlockSpec(memory_space=pltpu.SMEM)
F32, BF16 = jnp.float32, jnp.bfloat16
NT = (((1,), (1,)), ((), ()))


def swapped(block, axis, mask):
    size = lax.axis_size(axis)
    return lax.ppermute(block, axis, [(i, i ^ mask) for i in range(size)])


def dft_parts():
    freq = np.arange(SUB)[:, None]
    place = np.arange(SUB)[None, :]
    angle = (((2 * freq + 1) * place) % (4 * SUB)).astype(np.float64) * (math.pi / (2 * SUB))
    matrix = np.concatenate([np.cos(angle), -np.sin(angle)], axis=0).astype(np.float32)
    upper = matrix.astype(jnp.bfloat16)
    lower = (matrix - upper.astype(np.float32)).astype(jnp.bfloat16)
    return np.concatenate([upper, lower], axis=0), np.concatenate([upper.T, lower.T], axis=0)


def dot(a, b):
    return jnp.dot(a, b, preferred_element_type=F32)


def dot_parts(parts_ref, b):
    both = dot(parts_ref[...], b)
    half = both.shape[0] // 2
    return both[:half] + both[half:]


def prepare_kernel(widths, start_ref, w_ref, *refs):
    outs, sems = refs[:-1], refs[-1]
    copies = [
        pltpu.make_async_copy(
            w_ref.at[:, pl.ds(pl.multiple_of(start_ref[i], LANES), width)], outs[i], sems.at[i]
        )
        for i, width in enumerate(widths)
    ]
    for copy in copies:
        copy.start()
    for copy in copies:
        copy.wait()


def prepare(w_out, starts, widths):
    rows = w_out.shape[0]
    return pl.pallas_call(
        functools.partial(prepare_kernel, widths),
        out_shape=[jax.ShapeDtypeStruct((rows, width), w_out.dtype) for width in widths],
        in_specs=[SMEM, pl.BlockSpec(memory_space=pltpu.HBM)],
        out_specs=[VMEM] * len(widths),
        scratch_shapes=[pltpu.SemaphoreType.DMA((len(widths),))],
        compiler_params=pltpu.CompilerParams(vmem_limit_bytes=GRANT[0] << 20),
        cost_estimate=pl.CostEstimate(flops=0, bytes_accessed=4 << 20, transcendentals=0),
    )(jnp.stack(starts).astype(jnp.int32), w_out)


PIECES = 4


def hold_kernel(source_ref, out_ref, sems):
    rows = source_ref.shape[0] // PIECES
    copies = [
        pltpu.make_async_copy(source_ref.at[pl.ds(i * rows, rows)], out_ref.at[pl.ds(i * rows, rows)], sems.at[i])
        for i in range(PIECES)
    ]
    for copy in copies:
        copy.start()
    for copy in copies:
        copy.wait()


def hold(block):
    return pl.pallas_call(
        hold_kernel,
        out_shape=jax.ShapeDtypeStruct(block.shape, block.dtype),
        in_specs=[pl.BlockSpec(memory_space=pltpu.HBM)],
        out_specs=VMEM,
        scratch_shapes=[pltpu.SemaphoreType.DMA((PIECES,))],
        compiler_params=pltpu.CompilerParams(vmem_limit_bytes=GRANT[1] << 20),
        cost_estimate=pl.CostEstimate(flops=0, bytes_accessed=2 << 20, transcendentals=0),
    )(block)


def product_kernel(sizes, place_ref, d_ref, *refs):
    parts, outs = refs[: len(sizes)], refs[len(sizes) :]
    count = outs[0].shape[0]
    channels = outs[0].shape[-1]
    for i in range(0, count, 2):
        total = None
        for n, (part, (index, first, masks)) in enumerate(zip(parts, sizes)):
            if not first <= i < first + masks:
                continue
            width = part.shape[-1]
            start = pl.multiple_of(place_ref[n], width)
            w = jnp.concatenate([part[(*index, i - first)], part[(*index, i + 1 - first)]], axis=0)
            term = lax.dot_general(d_ref[:, pl.ds(start, width)], w, NT, preferred_element_type=F32)
            total = term if total is None else total + term
        for which in range(2):
            rows = slice(which * SUB, (which + 1) * SUB)
            outs[which][i] = total[rows, :channels].astype(outs[which].dtype)
            outs[which][i + 1] = total[rows, channels:].astype(outs[which].dtype)


def product(d_out, parts, out_type):
    count = max(first + block.shape[-3] for block, _, first, _ in parts)
    channels = parts[0][0].shape[-2]
    sizes = [(index, first, block.shape[-3]) for block, index, first, _ in parts]
    places = jnp.stack([start for _, _, _, start in parts]).astype(jnp.int32)
    return pl.pallas_call(
        functools.partial(product_kernel, sizes),
        out_shape=(jax.ShapeDtypeStruct((count, SUB, channels), out_type),) * 2,
        in_specs=[SMEM] + [VMEM] * (1 + len(parts)),
        out_specs=(VMEM, VMEM),
        compiler_params=pltpu.CompilerParams(vmem_limit_bytes=8 << 20),
        cost_estimate=pl.CostEstimate(
            flops=4 * count * SUB * channels * d_out.shape[1], bytes_accessed=4 << 20, transcendentals=0
        ),
    )(places, d_out, *[block for block, _, _, _ in parts])


def lag_kernel(n, seq_ref, dft_ref, *refs):
    blocks, out_ref, spec = refs[:n], refs[n], refs[n + 1]
    me = seq_ref[0]
    spec[0] = jnp.zeros_like(spec[0])
    out_ref[0] = jnp.zeros_like(out_ref[0])
    for offset in range(n):
        place = (me ^ offset) * 2 + 1
        for sub in range(2):
            rows = pl.ds(sub * SUB, SUB)
            data = jnp.concatenate([blocks[offset][0, rows, :], blocks[offset][1, rows, :]], axis=1)
            both = dot_parts(dft_ref, data)
            channels = data.shape[1] // 2
            spec[place + sub, 0] = both[:, :channels] * (1.0 / SUB)
            spec[place + sub, 1] = both[:, channels:] * (1.0 / SUB)
    channels = spec.shape[-1]
    sign = (1 - 2 * (lax.broadcasted_iota(jnp.int32, (SUB, channels), 0) % 2)).astype(F32)

    @pl.loop(0, 2 * n)
    def _(lag):
        for which in range(2):
            out_ref[lag + 1, which, :SUB] = spec[lag + 1, which, :SUB] - sign * spec[lag, which, SUB:]
            out_ref[lag + 1, which, SUB:] = spec[lag + 1, which, SUB:] + sign * spec[lag, which, :SUB]


def lag_spectra(seq_id, dft, blocks):
    n = len(blocks)
    channels = blocks[0].shape[-1]
    return pl.pallas_call(
        functools.partial(lag_kernel, n),
        out_shape=jax.ShapeDtypeStruct((2 * n + 1, 2, 2 * SUB, channels), F32),
        in_specs=[SMEM] + [VMEM] * (1 + n),
        out_specs=VMEM,
        scratch_shapes=[pltpu.VMEM((2 * n + 1, 2, 2 * SUB, channels), F32)],
        compiler_params=pltpu.CompilerParams(vmem_limit_bytes=(4 + 3 * n) << 20),
        cost_estimate=pl.CostEstimate(
            flops=16 * n * SUB * SUB * channels * 2, bytes_accessed=6 << 20, transcendentals=0
        ),
    )(seq_id, dft, *blocks)


CHUNK = 32
GRANT = (51, 52)


def add_kernel(offsets, which, first, last, seq_ref, dft_ref, lag_ref, *refs):
    blocks, refs = refs[: len(offsets)], list(refs[len(offsets) :])
    before = None if first else refs.pop(0)
    if last:
        back_ref, inner_ref, filter_ref, spec, total = refs
    else:
        total, spec = refs
    me = seq_ref[0]
    channels = spec.shape[-1]
    for pair in range(0, len(offsets), 2):
        used = offsets[pair : pair + 2]
        data = jnp.concatenate([blocks[pair + i][...] for i in range(len(used))], axis=1)
        both = dot_parts(dft_ref, data)
        for i in range(len(used)):
            spec[pair + i] = both[:, i * channels : (i + 1) * channels]

    for chunk in range(SUB // CHUNK):
        real, imag = pl.ds(chunk * CHUNK, CHUNK), pl.ds(SUB + chunk * CHUNK, CHUNK)
        sums = []
        for i in range(4):
            columns = slice(i * channels, (i + 1) * channels)
            zero = jnp.zeros((CHUNK, channels), F32)
            sums.append((zero, zero) if first else (before[real, columns], before[imag, columns]))
        for place, offset in enumerate(offsets):
            step = (me ^ offset) - me
            g_real, g_imag = spec[place, real, :], spec[place, imag, :]
            for i in range(4):
                array, sub = i // 2, i % 2
                lag = jnp.maximum(step * 2 + which - sub + 1, 0)
                k_real, k_imag = lag_ref[lag, array, real, :], lag_ref[lag, array, imag, :]
                s_real, s_imag = sums[i]
                s_real = s_real + g_real * k_real + g_imag * k_imag
                s_imag = s_imag + g_imag * k_real - g_real * k_imag
                sums[i] = (s_real, s_imag)
        for i in range(4):
            total[real, i * channels : (i + 1) * channels] = sums[i][0]
            total[imag, i * channels : (i + 1) * channels] = sums[i][1]
    if not last:
        return
    for array in range(2):
        whole = total[:, 2 * array * channels : 2 * (array + 1) * channels]
        high = whole.astype(BF16)
        low = (whole - high.astype(F32)).astype(BF16)
        values = dot_parts(back_ref, high) + dot(back_ref[:SUB, :], low)
        out_ref = (inner_ref, filter_ref)[array]
        out_ref[:SUB, :] = values[:, :channels].astype(out_ref.dtype)
        out_ref[SUB:, :] = values[:, channels:].astype(out_ref.dtype)


def add_blocks(n, seq_id, dft, lags, blocks, which, before=None, back=None):
    offsets = sorted(blocks)
    blocks = [blocks[offset] for offset in offsets]
    channels = blocks[0].shape[-1]
    first, last = before is None, back is not None
    whole = jax.ShapeDtypeStruct((2 * SUB, 4 * channels), F32)
    out_shape = whole
    scratch = [pltpu.VMEM((len(blocks), 2 * SUB, channels), F32)]
    if last:
        out_shape = (
            jax.ShapeDtypeStruct((2 * SUB, channels), BF16),
            jax.ShapeDtypeStruct((2 * SUB, channels), F32),
        )
        scratch.append(pltpu.VMEM(whole.shape, F32))
    args = (seq_id, dft, lags, *blocks) + (() if first else (before,)) + ((back,) if last else ())
    return pl.pallas_call(
        functools.partial(add_kernel, offsets, which, first, last),
        out_shape=out_shape,
        in_specs=[SMEM] + [VMEM] * (len(args) - 1),
        out_specs=(VMEM, VMEM) if last else VMEM,
        scratch_shapes=scratch,
        compiler_params=pltpu.CompilerParams(vmem_limit_bytes=(6 + 2 * n) << 20),
        cost_estimate=pl.CostEstimate(
            flops=8 * len(blocks) * SUB * SUB * channels * 2, bytes_accessed=4 << 20, transcendentals=0
        ),
    )(*args)


def spread_offsets(size):
    held, moves, mask = [0], [], size // 2
    while mask:
        new = [(offset | mask, offset, mask) for offset in held]
        moves += new
        held += [offset for offset, _, _ in new]
        mask //= 2
    return moves


def spread_blocks(block, axis):
    size = lax.axis_size(axis)
    held = {0: block}
    for offset, source, mask in spread_offsets(size):
        held[offset] = swapped(held[source], axis, mask)
    return held


def masks_of(chan_n):
    odd = [m for m in reversed(range(chan_n)) if m % 2]
    return odd, [m - 1 for m in odd]


def far_count(chan_n, features):
    return chan_n // 4 if features % (4 * LANES) == 0 else 0


def body(d_out, w_out, gate, inner, filt):
    chan_n = lax.axis_size("chan")
    seq, chan = lax.axis_index("seq"), lax.axis_index("chan")
    core, side = seq % 2, seq // 2 % 2
    seq_id = seq.astype(jnp.int32)[None]
    features = d_out.shape[1]
    half, quarter = features // 2, features // 4
    odd, even = masks_of(chan_n)
    groups = chan_n // 2
    far = far_count(chan_n, features)

    def place(mask, split):
        return (chan ^ mask) * features + core * half + (side * quarter if split else 0)

    splits = [i < far for i in range(groups)]
    starts = [place(mask, split) for mask, split in zip(odd + even, splits + [False] * groups)]
    starts.append(chan * features + (1 - core) * half)
    blocks = list(prepare(w_out, starts, [quarter if split else half for split in splits] + [half] * (groups + 1)))
    d_out = hold(d_out)
    for i, mask in enumerate(odd + even[:-1]):
        blocks[i] = swapped(blocks[i], "chan", mask)
    odd_parts, even_parts = [], []
    if far:
        own = jnp.stack(blocks[:far])
        own = jnp.stack([own, swapped(own, "seq", 2)])
        twin = swapped(own, "seq", 1)
        for other_core, block in enumerate((own, twin)):
            for other_side in range(2):
                start = (core ^ other_core) * half + (side ^ other_side) * quarter
                odd_parts.append((block, (other_side,), 0, start))
    near = jnp.stack(blocks[far:groups])
    twin = swapped(near, "seq", 1)
    odd_parts += [(near, (), far, core * half), (twin, (), far, (1 - core) * half)]
    lag_pair = jnp.stack([filt, inner])
    lag_blocks = [block for _, block in sorted(spread_blocks(lag_pair, "seq").items())]
    dft, back = dft_parts()

    p_odd = product(d_out, odd_parts, BF16)
    *later, _ = lax.optimization_barrier((*blocks[groups : 2 * groups - 1], p_odd[0]))
    near = jnp.stack(later)
    twin = swapped(near, "seq", 1)
    even_parts = [
        (jnp.concatenate([near, blocks[-2][None]]), (), 0, core * half),
        (jnp.concatenate([twin, blocks[-1][None]]), (), 0, (1 - core) * half),
    ]
    from_pair = [swapped(p_odd[which], "chan", 1) for which in range(2)]
    lags = lag_spectra(seq_id, dft, lag_blocks)
    p_even = product(d_out, even_parts, F32)
    sums, sent = [], []
    for which in range(2):
        sums.append([p_even[which][i] + from_pair[which][i].astype(F32) for i in range(groups)])
        sent.append([block.astype(BF16) for block in sums[which][:-1]])
    parts = [[swapped(block, "chan", mask) for block, mask in zip(sent[which], even)] for which in range(2)]
    tied = lax.optimization_barrier((*parts[0], *sent[1]))
    parts[0] = list(tied[: groups - 1])
    grad_blocks = []
    for which in range(2):
        grad_gated = sums[which][-1]
        for part in parts[which]:
            grad_gated = grad_gated + part.astype(F32)
        gate_part = gate[which * SUB : (which + 1) * SUB].astype(F32)
        grad_conv = (gate_part * grad_gated).astype(BF16)
        gate, grad_conv = lax.optimization_barrier((gate, grad_conv))
        grad_blocks.append(spread_blocks(grad_conv, "seq"))
    seq_n = lax.axis_size("seq")
    groups_of = stages(seq_n)
    total = None
    for i, (which, offsets) in enumerate(groups_of):
        last = i == len(groups_of) - 1
        chosen = {offset: grad_blocks[which][offset] for offset in offsets}
        total = add_blocks(seq_n, seq_id, dft, lags, chosen, which, total, back if last else None)
    return tuple(total)


def stages(seq_n):
    near = [0, 1] if seq_n > 1 else [0]
    rest = [offset for offset in range(seq_n) if offset not in near]
    return [(0, list(range(seq_n))), (1, near)] + ([(1, rest)] if rest else [])


def solution(mesh):
    placed = (
        P("seq", "chan"),
        P("chan", None),
        P("seq", "chan"),
        P("seq", "chan"),
        P("seq", "chan"),
    )

    return jax.shard_map(
        body,
        mesh=mesh,
        in_specs=placed,
        out_specs=(P("seq", "chan"), P("seq", "chan")),
        check_vma=False,
    )
```

```python
import functools
import math

import jax
import jax.numpy as jnp
import numpy as np
from jax import lax
from jax.experimental import pallas as pl
from jax.experimental.pallas import tpu as pltpu
from jax.sharding import PartitionSpec as P


SUB = 256
LANES = 128
VMEM = pl.BlockSpec(memory_space=pltpu.VMEM)
F32, BF16 = jnp.float32, jnp.bfloat16
NT = (((1,), (1,)), ((), ()))


def swapped(block, axis, mask):
    size = lax.axis_size(axis)
    return lax.ppermute(block, axis, [(i, i ^ mask) for i in range(size)])


def dft_parts():
    freq = np.arange(SUB)[:, None]
    place = np.arange(SUB)[None, :]
    angle = (((2 * freq + 1) * place) % (4 * SUB)).astype(np.float64) * (math.pi / (2 * SUB))
    matrix = np.concatenate([np.cos(angle), -np.sin(angle)], axis=0).astype(np.float32)
    upper = matrix.astype(jnp.bfloat16)
    lower = (matrix - upper.astype(np.float32)).astype(jnp.bfloat16)
    return np.concatenate([upper, lower], axis=0), np.concatenate([upper.T, lower.T], axis=0)


def dot(a, b):
    return jnp.dot(a, b, preferred_element_type=F32)


def dot_parts(parts_ref, b):
    both = dot(parts_ref[...], b)
    half = both.shape[0] // 2
    return both[:half] + both[half:]


def prepare_kernel(features, wanted, w_ref, *refs):
    outs, sems = refs[:-1], refs[-1]
    chan = lax.axis_index("chan")
    copies = []
    for i, (mask, split, other_core) in enumerate(wanted):
        width = outs[i].shape[-1]
        start = (chan ^ mask) * features + start_of(features, split, other_core, 0)
        source = w_ref.at[:, pl.ds(pl.multiple_of(start, width), width)]
        copies.append(pltpu.make_async_copy(source, outs[i], sems.at[i]))
    for copy in copies:
        copy.start()
    for copy in copies:
        copy.wait()


def prepare(w_out, features, wanted):
    rows = w_out.shape[0]
    widths = [features // (4 if split else 2) for _, split, _ in wanted]
    return pl.pallas_call(
        functools.partial(prepare_kernel, features, wanted),
        out_shape=[jax.ShapeDtypeStruct((rows, width), w_out.dtype) for width in widths],
        in_specs=[pl.BlockSpec(memory_space=pltpu.HBM)],
        out_specs=[VMEM] * len(widths),
        scratch_shapes=[pltpu.SemaphoreType.DMA((len(widths),))],
        compiler_params=pltpu.CompilerParams(vmem_limit_bytes=GRANT[0] << 20),
        cost_estimate=pl.CostEstimate(flops=0, bytes_accessed=4 << 20, transcendentals=0),
    )(w_out)


PIECES = 4


def hold_kernel(source_ref, out_ref, sems):
    rows = source_ref.shape[0] // PIECES
    copies = [
        pltpu.make_async_copy(source_ref.at[pl.ds(i * rows, rows)], out_ref.at[pl.ds(i * rows, rows)], sems.at[i])
        for i in range(PIECES)
    ]
    for copy in copies:
        copy.start()
    for copy in copies:
        copy.wait()


def hold(block):
    return pl.pallas_call(
        hold_kernel,
        out_shape=jax.ShapeDtypeStruct(block.shape, block.dtype),
        in_specs=[pl.BlockSpec(memory_space=pltpu.HBM)],
        out_specs=VMEM,
        scratch_shapes=[pltpu.SemaphoreType.DMA((PIECES,))],
        compiler_params=pltpu.CompilerParams(vmem_limit_bytes=GRANT[1] << 20),
        cost_estimate=pl.CostEstimate(flops=0, bytes_accessed=2 << 20, transcendentals=0),
    )(block)


def start_of(features, split, other_core, other_side):
    seq = lax.axis_index("seq")
    core, side = (seq & 1) ^ other_core, ((seq >> 1) & 1) ^ other_side
    return core * (features // 2) + (side * (features // 4) if split else 0)


def product_kernel(sizes, d_ref, *refs):
    parts, outs = refs[: len(sizes)], refs[len(sizes) :]
    count = outs[0].shape[0]
    channels = outs[0].shape[-1]
    for which in range(2):
        rows = pl.ds(which * SUB, SUB)
        lefts = []
        for part, (_, _, _, whose) in zip(parts, sizes):
            width = part.shape[-1]
            start = pl.multiple_of(start_of(d_ref.shape[1], *whose), width)
            lefts.append(d_ref[rows, pl.ds(start, width)])
        for i in range(0, count, 2):
            total = None
            for left, part, (index, first, masks, _) in zip(lefts, parts, sizes):
                if not first <= i < first + masks:
                    continue
                w = jnp.concatenate([part[(*index, i - first)], part[(*index, i + 1 - first)]], axis=0)
                term = lax.dot_general(left, w, NT, preferred_element_type=F32)
                total = term if total is None else total + term
            outs[which][i] = total[:, :channels].astype(outs[which].dtype)
            outs[which][i + 1] = total[:, channels:].astype(outs[which].dtype)


def product(d_out, parts, out_type):
    count = max(first + block.shape[-3] for block, _, first, _ in parts)
    channels = parts[0][0].shape[-2]
    sizes = [(index, first, block.shape[-3], whose) for block, index, first, whose in parts]
    return pl.pallas_call(
        functools.partial(product_kernel, sizes),
        out_shape=(jax.ShapeDtypeStruct((count, SUB, channels), out_type),) * 2,
        in_specs=[VMEM] * (1 + len(parts)),
        out_specs=(VMEM, VMEM),
        compiler_params=pltpu.CompilerParams(vmem_limit_bytes=8 << 20),
        cost_estimate=pl.CostEstimate(
            flops=4 * count * SUB * channels * d_out.shape[1], bytes_accessed=4 << 20, transcendentals=0
        ),
    )(d_out, *[block for block, _, _, _ in parts])


def lag_kernel(n, dft_ref, *refs):
    blocks, out_ref, spec = refs[:n], refs[n], refs[n + 1]
    me = lax.axis_index("seq")
    spec[0] = jnp.zeros_like(spec[0])
    out_ref[0] = jnp.zeros_like(out_ref[0])
    for offset in range(n):
        place = (me ^ offset) * 2 + 1
        for sub in range(2):
            rows = pl.ds(sub * SUB, SUB)
            data = jnp.concatenate([blocks[offset][0, rows, :], blocks[offset][1, rows, :]], axis=1)
            both = dot_parts(dft_ref, data)
            channels = data.shape[1] // 2
            spec[place + sub, 0] = both[:, :channels] * (1.0 / SUB)
            spec[place + sub, 1] = both[:, channels:] * (1.0 / SUB)
    channels = spec.shape[-1]
    sign = (1 - 2 * (lax.broadcasted_iota(jnp.int32, (SUB, channels), 0) % 2)).astype(F32)

    @pl.loop(0, 2 * n)
    def _(lag):
        for which in range(2):
            out_ref[lag + 1, which, :SUB] = spec[lag + 1, which, :SUB] - sign * spec[lag, which, SUB:]
            out_ref[lag + 1, which, SUB:] = spec[lag + 1, which, SUB:] + sign * spec[lag, which, :SUB]


def lag_spectra(dft, blocks):
    n = len(blocks)
    channels = blocks[0].shape[-1]
    return pl.pallas_call(
        functools.partial(lag_kernel, n),
        out_shape=jax.ShapeDtypeStruct((2 * n + 1, 2, 2 * SUB, channels), F32),
        in_specs=[VMEM] * (1 + n),
        out_specs=VMEM,
        scratch_shapes=[pltpu.VMEM((2 * n + 1, 2, 2 * SUB, channels), F32)],
        compiler_params=pltpu.CompilerParams(vmem_limit_bytes=(4 + 3 * n) << 20),
        cost_estimate=pl.CostEstimate(
            flops=16 * n * SUB * SUB * channels * 2, bytes_accessed=6 << 20, transcendentals=0
        ),
    )(dft, *blocks)


CHUNK = 32
GRANT = (51, 52)


def add_kernel(offsets, which, first, last, dft_ref, lag_ref, *refs):
    blocks, refs = refs[: len(offsets)], list(refs[len(offsets) :])
    before = None if first else refs.pop(0)
    if last:
        back_ref, inner_ref, filter_ref, spec, total = refs
    else:
        total, spec = refs
    me = lax.axis_index("seq")
    channels = spec.shape[-1]
    for pair in range(0, len(offsets), 2):
        used = offsets[pair : pair + 2]
        data = jnp.concatenate([blocks[pair + i][...] for i in range(len(used))], axis=1)
        both = dot_parts(dft_ref, data)
        for i in range(len(used)):
            spec[pair + i] = both[:, i * channels : (i + 1) * channels]

    for array in range(2):
        for chunk in range(SUB // CHUNK):
            real, imag = pl.ds(chunk * CHUNK, CHUNK), pl.ds(SUB + chunk * CHUNK, CHUNK)
            places = [slice((2 * array + sub) * channels, (2 * array + sub + 1) * channels) for sub in range(2)]
            zero = jnp.zeros((CHUNK, channels), F32)
            sums = [(zero, zero) if first else (before[real, p], before[imag, p]) for p in places]
            for place, offset in enumerate(offsets):
                step = (me ^ offset) - me
                g_real, g_imag = spec[place, real, :], spec[place, imag, :]
                for sub in range(2):
                    lag = jnp.maximum(step * 2 + which - sub + 1, 0)
                    k_real, k_imag = lag_ref[lag, array, real, :], lag_ref[lag, array, imag, :]
                    s_real, s_imag = sums[sub]
                    s_real = s_real + g_real * k_real + g_imag * k_imag
                    s_imag = s_imag + g_imag * k_real - g_real * k_imag
                    sums[sub] = (s_real, s_imag)
            for p, (s_real, s_imag) in zip(places, sums):
                total[real, p] = s_real
                total[imag, p] = s_imag
        if not last:
            continue
        whole = total[:, 2 * array * channels : 2 * (array + 1) * channels]
        high = whole.astype(BF16)
        low = (whole - high.astype(F32)).astype(BF16)
        values = dot_parts(back_ref, high) + dot(back_ref[:SUB, :], low)
        out_ref = (inner_ref, filter_ref)[array]
        out_ref[:SUB, :] = values[:, :channels].astype(out_ref.dtype)
        out_ref[SUB:, :] = values[:, channels:].astype(out_ref.dtype)


def add_blocks(n, dft, lags, blocks, which, before=None, back=None):
    offsets = sorted(blocks)
    blocks = [blocks[offset] for offset in offsets]
    channels = blocks[0].shape[-1]
    first, last = before is None, back is not None
    whole = jax.ShapeDtypeStruct((2 * SUB, 4 * channels), F32)
    out_shape = whole
    scratch = [pltpu.VMEM((len(blocks), 2 * SUB, channels), F32)]
    if last:
        out_shape = (
            jax.ShapeDtypeStruct((2 * SUB, channels), BF16),
            jax.ShapeDtypeStruct((2 * SUB, channels), F32),
        )
        scratch.append(pltpu.VMEM(whole.shape, F32))
    args = (dft, lags, *blocks) + (() if first else (before,)) + ((back,) if last else ())
    return pl.pallas_call(
        functools.partial(add_kernel, offsets, which, first, last),
        out_shape=out_shape,
        in_specs=[VMEM] * len(args),
        out_specs=(VMEM, VMEM) if last else VMEM,
        scratch_shapes=scratch,
        compiler_params=pltpu.CompilerParams(vmem_limit_bytes=(6 + 2 * n) << 20),
        cost_estimate=pl.CostEstimate(
            flops=8 * len(blocks) * SUB * SUB * channels * 2, bytes_accessed=4 << 20, transcendentals=0
        ),
    )(*args)


def spread_offsets(size):
    if size <= 4:
        return [(offset, 0, offset) for offset in reversed(range(1, size))]
    held, moves, mask = [0], [], size // 2
    while mask:
        new = [(offset | mask, offset, mask) for offset in held]
        moves += new
        held += [offset for offset, _, _ in new]
        mask //= 2
    return moves


def spread_blocks(block, axis):
    size = lax.axis_size(axis)
    held = {0: block}
    for offset, source, mask in spread_offsets(size):
        held[offset] = swapped(held[source], axis, mask)
    return held


def masks_of(chan_n):
    odd = [m for m in reversed(range(chan_n)) if m % 2]
    return odd, [m - 1 for m in odd]


def far_count(chan_n, features):
    return chan_n // 4 if features % (4 * LANES) == 0 else 0


def body(d_out, w_out, gate, inner, filt):
    chan_n = lax.axis_size("chan")
    features = d_out.shape[1]
    odd, even = masks_of(chan_n)
    groups = chan_n // 2
    far = far_count(chan_n, features)

    wanted = [(mask, i < far, 0) for i, mask in enumerate(odd)] + [(mask, False, 0) for mask in even] + [(0, False, 1)]
    blocks = list(prepare(w_out, features, wanted))
    d_out = hold(d_out)
    for i, mask in enumerate(odd + even[:-1]):
        blocks[i] = swapped(blocks[i], "chan", mask)
    odd_parts, even_parts = [], []
    if far:
        sides = [swapped(blocks[i], "seq", 2) for i in range(far)]
        owns = [jnp.stack([blocks[i], sides[i]]) for i in range(far)]
        twins = [swapped(owns[i], "seq", 1) for i in range(far)]
        for other_core, block in enumerate((jnp.stack(owns, axis=1), jnp.stack(twins, axis=1))):
            for other_side in range(2):
                odd_parts.append((block, (other_side,), 0, (True, other_core, other_side)))
    near = jnp.stack(blocks[far:groups])
    twin = swapped(near, "seq", 1)
    odd_parts += [(near, (), far, (False, 0, 0)), (twin, (), far, (False, 1, 0))]
    lag_pair = jnp.stack([filt, inner])
    lag_blocks = [block for _, block in sorted(spread_blocks(lag_pair, "seq").items())]
    dft, back = dft_parts()

    p_odd = product(d_out, odd_parts, BF16)
    *later, _ = lax.optimization_barrier((*blocks[groups : 2 * groups - 1], p_odd[0]))
    near = jnp.stack(later)
    twin = swapped(near, "seq", 1)
    even_parts = [
        (jnp.concatenate([near, blocks[-2][None]]), (), 0, (False, 0, 0)),
        (jnp.concatenate([twin, blocks[-1][None]]), (), 0, (False, 1, 0)),
    ]
    from_pair = [swapped(p_odd[which], "chan", 1) for which in range(2)]
    lags = lag_spectra(dft, lag_blocks)
    p_even = product(d_out, even_parts, F32)
    own, parts = [], []
    for which in range(2):
        mine, theirs = p_even[which], from_pair[which]
        sent = []
        for i, mask in enumerate(even):
            if which and i == groups - 2:
                mine, theirs, *_ = lax.optimization_barrier((mine, theirs, *sent))
            total = mine[i] + theirs[i].astype(F32)
            sent.append(total.astype(BF16) if mask else total)
        own.append(sent.pop())
        parts.append([swapped(block, "chan", mask) for block, mask in zip(sent, even)])
    grad_blocks = []
    for which in range(2):
        grad_gated = own[which]
        for part in parts[which]:
            grad_gated = grad_gated + part.astype(F32)
        gate_part = gate[which * SUB : (which + 1) * SUB].astype(F32)
        grad_conv = (gate_part * grad_gated).astype(BF16)
        gate, grad_conv = lax.optimization_barrier((gate, grad_conv))
        grad_blocks.append(spread_blocks(grad_conv, "seq"))
    seq_n = lax.axis_size("seq")
    groups_of = stages(seq_n)
    total = None
    for i, (which, offsets) in enumerate(groups_of):
        last = i == len(groups_of) - 1
        chosen = {offset: grad_blocks[which][offset] for offset in offsets}
        total = add_blocks(seq_n, dft, lags, chosen, which, total, back if last else None)
    return tuple(total)


def stages(seq_n):
    near = [0, 1] if seq_n > 1 else [0]
    rest = [offset for offset in range(seq_n) if offset not in near]
    return [(0, list(range(seq_n))), (1, near)] + ([(1, rest)] if rest else [])


def solution(mesh):
    placed = (
        P("seq", "chan"),
        P("chan", None),
        P("seq", "chan"),
        P("seq", "chan"),
        P("seq", "chan"),
    )

    return jax.shard_map(
        body,
        mesh=mesh,
        in_specs=placed,
        out_specs=(P("seq", "chan"), P("seq", "chan")),
        check_vma=False,
    )
```

```python
import functools
import math

import jax
import jax.numpy as jnp
import numpy as np
from jax import lax
from jax.experimental import pallas as pl
from jax.experimental.pallas import tpu as pltpu
from jax.sharding import PartitionSpec as P


SUB = 256
LANES = 128
VMEM = pl.BlockSpec(memory_space=pltpu.VMEM)
F32, BF16 = jnp.float32, jnp.bfloat16
NT = (((1,), (1,)), ((), ()))


def swapped(block, axis, mask):
    size = lax.axis_size(axis)
    return lax.ppermute(block, axis, [(i, i ^ mask) for i in range(size)])


def dft_parts():
    freq = np.arange(SUB)[:, None]
    place = np.arange(SUB)[None, :]
    angle = (((2 * freq + 1) * place) % (4 * SUB)).astype(np.float64) * (math.pi / (2 * SUB))
    matrix = np.concatenate([np.cos(angle), -np.sin(angle)], axis=0).astype(np.float32)
    upper = matrix.astype(jnp.bfloat16)
    lower = (matrix - upper.astype(np.float32)).astype(jnp.bfloat16)
    return np.concatenate([upper, lower], axis=0), np.concatenate([upper.T, lower.T], axis=0)


def dot(a, b):
    return jnp.dot(a, b, preferred_element_type=F32)


def dot_parts(parts_ref, b):
    both = dot(parts_ref[...], b)
    half = both.shape[0] // 2
    return both[:half] + both[half:]


def prepare_kernel(features, wanted, w_ref, *refs):
    outs, sems = refs[:-1], refs[-1]
    chan = lax.axis_index("chan")
    copies = []
    for i, (mask, split, other_core) in enumerate(wanted):
        width = outs[i].shape[-1]
        start = (chan ^ mask) * features + start_of(features, split, other_core, 0)
        source = w_ref.at[:, pl.ds(pl.multiple_of(start, width), width)]
        copies.append(pltpu.make_async_copy(source, outs[i], sems.at[i]))
    for copy in copies:
        copy.start()
    for copy in copies:
        copy.wait()


def prepare(w_out, features, wanted):
    rows = w_out.shape[0]
    widths = [features // (4 if split else 2) for _, split, _ in wanted]
    return pl.pallas_call(
        functools.partial(prepare_kernel, features, wanted),
        out_shape=[jax.ShapeDtypeStruct((rows, width), w_out.dtype) for width in widths],
        in_specs=[pl.BlockSpec(memory_space=pltpu.HBM)],
        out_specs=[VMEM] * len(widths),
        scratch_shapes=[pltpu.SemaphoreType.DMA((len(widths),))],
        compiler_params=pltpu.CompilerParams(vmem_limit_bytes=GRANT[0] << 20),
        cost_estimate=pl.CostEstimate(flops=0, bytes_accessed=4 << 20, transcendentals=0),
    )(w_out)


PIECES = 4


def hold_kernel(source_ref, out_ref, sems):
    rows = source_ref.shape[0] // PIECES
    copies = [
        pltpu.make_async_copy(source_ref.at[pl.ds(i * rows, rows)], out_ref.at[pl.ds(i * rows, rows)], sems.at[i])
        for i in range(PIECES)
    ]
    for copy in copies:
        copy.start()
    for copy in copies:
        copy.wait()


def hold(block):
    return pl.pallas_call(
        hold_kernel,
        out_shape=jax.ShapeDtypeStruct(block.shape, block.dtype),
        in_specs=[pl.BlockSpec(memory_space=pltpu.HBM)],
        out_specs=VMEM,
        scratch_shapes=[pltpu.SemaphoreType.DMA((PIECES,))],
        compiler_params=pltpu.CompilerParams(vmem_limit_bytes=GRANT[1] << 20),
        cost_estimate=pl.CostEstimate(flops=0, bytes_accessed=2 << 20, transcendentals=0),
    )(block)


def start_of(features, split, other_core, other_side):
    seq = lax.axis_index("seq")
    core, side = (seq & 1) ^ other_core, ((seq >> 1) & 1) ^ other_side
    return core * (features // 2) + (side * (features // 4) if split else 0)


def product_kernel(sizes, d_ref, *refs):
    parts, outs = refs[: len(sizes)], refs[len(sizes) :]
    count = 2 * outs[0].shape[0]
    channels = outs[0].shape[-1]
    for which in range(2):
        rows = pl.ds(which * SUB, SUB)
        lefts = []
        for part, (_, _, _, whose) in zip(parts, sizes):
            width = part.shape[-1]
            start = pl.multiple_of(start_of(d_ref.shape[1], *whose), width)
            lefts.append(d_ref[rows, pl.ds(start, width)])
        for i in range(0, count, 2):
            total = None
            for left, part, (index, first, masks, _) in zip(lefts, parts, sizes):
                if not first <= i < first + masks:
                    continue
                w = jnp.concatenate([part[(*index, i - first)], part[(*index, i + 1 - first)]], axis=0)
                term = lax.dot_general(left, w, NT, preferred_element_type=F32)
                total = term if total is None else total + term
            out_ref, at = outs[2 * which + 2 * i // count], i % (count // 2)
            out_ref[at] = total[:, :channels].astype(out_ref.dtype)
            out_ref[at + 1] = total[:, channels:].astype(out_ref.dtype)


def product(d_out, parts, out_type):
    count = max(first + block.shape[-3] for block, _, first, _ in parts)
    channels = parts[0][0].shape[-2]
    sizes = [(index, first, block.shape[-3], whose) for block, index, first, whose in parts]
    return pl.pallas_call(
        functools.partial(product_kernel, sizes),
        out_shape=(jax.ShapeDtypeStruct((count // 2, SUB, channels), out_type),) * 4,
        in_specs=[VMEM] * (1 + len(parts)),
        out_specs=(VMEM,) * 4,
        compiler_params=pltpu.CompilerParams(vmem_limit_bytes=8 << 20),
        cost_estimate=pl.CostEstimate(
            flops=4 * count * SUB * channels * d_out.shape[1], bytes_accessed=4 << 20, transcendentals=0
        ),
    )(d_out, *[block for block, _, _, _ in parts])


def lag_kernel(n, dft_ref, *refs):
    blocks, out_ref, spec = refs[:n], refs[n], refs[n + 1]
    me = lax.axis_index("seq")
    spec[0] = jnp.zeros_like(spec[0])
    out_ref[0] = jnp.zeros_like(out_ref[0])
    for offset in range(n):
        place = (me ^ offset) * 2 + 1
        for sub in range(2):
            rows = pl.ds(sub * SUB, SUB)
            data = jnp.concatenate([blocks[offset][0, rows, :], blocks[offset][1, rows, :]], axis=1)
            both = dot_parts(dft_ref, data)
            channels = data.shape[1] // 2
            spec[place + sub, 0] = both[:, :channels] * (1.0 / SUB)
            spec[place + sub, 1] = both[:, channels:] * (1.0 / SUB)
    channels = spec.shape[-1]
    sign = (1 - 2 * (lax.broadcasted_iota(jnp.int32, (SUB, channels), 0) % 2)).astype(F32)

    @pl.loop(0, 2 * n)
    def _(lag):
        for which in range(2):
            out_ref[lag + 1, which, :SUB] = spec[lag + 1, which, :SUB] - sign * spec[lag, which, SUB:]
            out_ref[lag + 1, which, SUB:] = spec[lag + 1, which, SUB:] + sign * spec[lag, which, :SUB]


def lag_spectra(dft, blocks):
    n = len(blocks)
    channels = blocks[0].shape[-1]
    return pl.pallas_call(
        functools.partial(lag_kernel, n),
        out_shape=jax.ShapeDtypeStruct((2 * n + 1, 2, 2 * SUB, channels), F32),
        in_specs=[VMEM] * (1 + n),
        out_specs=VMEM,
        scratch_shapes=[pltpu.VMEM((2 * n + 1, 2, 2 * SUB, channels), F32)],
        compiler_params=pltpu.CompilerParams(vmem_limit_bytes=(4 + 3 * n) << 20),
        cost_estimate=pl.CostEstimate(
            flops=16 * n * SUB * SUB * channels * 2, bytes_accessed=6 << 20, transcendentals=0
        ),
    )(dft, *blocks)


CHUNK = 32
GRANT = (51, 52)


def add_kernel(offsets, which, first, last, dft_ref, lag_ref, *refs):
    blocks, refs = refs[: len(offsets)], list(refs[len(offsets) :])
    before = None if first else refs.pop(0)
    if last:
        back_ref, inner_ref, filter_ref, spec, total = refs
    else:
        total, spec = refs
    me = lax.axis_index("seq")
    channels = spec.shape[-1]
    for pair in range(0, len(offsets), 2):
        used = offsets[pair : pair + 2]
        data = jnp.concatenate([blocks[pair + i][...] for i in range(len(used))], axis=1)
        both = dot_parts(dft_ref, data)
        for i in range(len(used)):
            spec[pair + i] = both[:, i * channels : (i + 1) * channels]

    for array in range(2):
        for chunk in range(SUB // CHUNK):
            real, imag = pl.ds(chunk * CHUNK, CHUNK), pl.ds(SUB + chunk * CHUNK, CHUNK)
            places = [slice((2 * array + sub) * channels, (2 * array + sub + 1) * channels) for sub in range(2)]
            zero = jnp.zeros((CHUNK, channels), F32)
            sums = [(zero, zero) if first else (before[real, p], before[imag, p]) for p in places]
            for place, offset in enumerate(offsets):
                step = (me ^ offset) - me
                g_real, g_imag = spec[place, real, :], spec[place, imag, :]
                for sub in range(2):
                    lag = jnp.maximum(step * 2 + which - sub + 1, 0)
                    k_real, k_imag = lag_ref[lag, array, real, :], lag_ref[lag, array, imag, :]
                    s_real, s_imag = sums[sub]
                    s_real = s_real + g_real * k_real + g_imag * k_imag
                    s_imag = s_imag + g_imag * k_real - g_real * k_imag
                    sums[sub] = (s_real, s_imag)
            for p, (s_real, s_imag) in zip(places, sums):
                total[real, p] = s_real
                total[imag, p] = s_imag
        if not last:
            continue
        whole = total[:, 2 * array * channels : 2 * (array + 1) * channels]
        high = whole.astype(BF16)
        low = (whole - high.astype(F32)).astype(BF16)
        values = dot_parts(back_ref, high) + dot(back_ref[:SUB, :], low)
        out_ref = (inner_ref, filter_ref)[array]
        out_ref[:SUB, :] = values[:, :channels].astype(out_ref.dtype)
        out_ref[SUB:, :] = values[:, channels:].astype(out_ref.dtype)


def add_blocks(n, dft, lags, blocks, which, before=None, back=None):
    offsets = sorted(blocks)
    blocks = [blocks[offset] for offset in offsets]
    channels = blocks[0].shape[-1]
    first, last = before is None, back is not None
    whole = jax.ShapeDtypeStruct((2 * SUB, 4 * channels), F32)
    out_shape = whole
    scratch = [pltpu.VMEM((len(blocks), 2 * SUB, channels), F32)]
    if last:
        out_shape = (
            jax.ShapeDtypeStruct((2 * SUB, channels), BF16),
            jax.ShapeDtypeStruct((2 * SUB, channels), F32),
        )
        scratch.append(pltpu.VMEM(whole.shape, F32))
    args = (dft, lags, *blocks) + (() if first else (before,)) + ((back,) if last else ())
    return pl.pallas_call(
        functools.partial(add_kernel, offsets, which, first, last),
        out_shape=out_shape,
        in_specs=[VMEM] * len(args),
        out_specs=(VMEM, VMEM) if last else VMEM,
        scratch_shapes=scratch,
        compiler_params=pltpu.CompilerParams(vmem_limit_bytes=(6 + 2 * n) << 20),
        cost_estimate=pl.CostEstimate(
            flops=8 * len(blocks) * SUB * SUB * channels * 2, bytes_accessed=4 << 20, transcendentals=0
        ),
    )(*args)


def spread_offsets(size, direct=True):
    if direct and size <= 4:
        return [(offset, 0, offset) for offset in reversed(range(1, size))]
    held, moves, mask = [0], [], size // 2
    while mask:
        new = [(offset | mask, offset, mask) for offset in held]
        moves += new
        held += [offset for offset, _, _ in new]
        mask //= 2
    return moves


def spread_blocks(block, axis, direct=True):
    size = lax.axis_size(axis)
    held = {0: block}
    for offset, source, mask in spread_offsets(size, direct):
        held[offset] = swapped(held[source], axis, mask)
    return held


def masks_of(chan_n):
    odd = [m for m in reversed(range(chan_n)) if m % 2]
    return odd, [m - 1 for m in odd]


def far_count(chan_n, features):
    return chan_n // 4 if features % (4 * LANES) == 0 else 0


def body(d_out, w_out, gate, inner, filt):
    chan_n = lax.axis_size("chan")
    features = d_out.shape[1]
    odd, even = masks_of(chan_n)
    groups = chan_n // 2
    far = far_count(chan_n, features)

    wanted = [(mask, i < far, 0) for i, mask in enumerate(odd)] + [(mask, False, 0) for mask in even] + [(0, False, 1)]
    blocks = list(prepare(w_out, features, wanted))
    d_out = hold(d_out)
    for i, mask in enumerate(odd + even[:-1]):
        blocks[i] = swapped(blocks[i], "chan", mask)
    odd_parts, even_parts = [], []
    if far:
        sides = [swapped(blocks[i], "seq", 2) for i in range(far)]
        owns = [jnp.stack([blocks[i], sides[i]]) for i in range(far)]
        twins = [swapped(owns[i], "seq", 1) for i in range(far)]
        for other_core, block in enumerate((jnp.stack(owns, axis=1), jnp.stack(twins, axis=1))):
            for other_side in range(2):
                odd_parts.append((block, (other_side,), 0, (True, other_core, other_side)))
    near = jnp.stack(blocks[far:groups])
    twin = swapped(near, "seq", 1)
    odd_parts += [(near, (), far, (False, 0, 0)), (twin, (), far, (False, 1, 0))]
    lag_pair = jnp.stack([filt, inner])
    lag_blocks = [block for _, block in sorted(spread_blocks(lag_pair, "seq", False).items())]
    dft, back = dft_parts()

    p_odd = product(d_out, odd_parts, BF16)
    *later, _ = lax.optimization_barrier((*blocks[groups : 2 * groups - 1], p_odd[0]))
    near = jnp.stack(later)
    twin = swapped(near, "seq", 1)
    even_parts = [
        (jnp.concatenate([near, blocks[-2][None]]), (), 0, (False, 0, 0)),
        (jnp.concatenate([twin, blocks[-1][None]]), (), 0, (False, 1, 0)),
    ]
    from_pair = [swapped(block, "chan", 1) for block in p_odd]
    lags = lag_spectra(dft, lag_blocks)
    p_even = product(d_out, even_parts, F32)
    own, parts, size = [], [], groups // 2
    for which in range(2):
        sent = []
        for kind in range(2):
            mine, theirs = p_even[2 * which + kind], from_pair[2 * which + kind]
            totals = [mine[i] + theirs[i].astype(F32) for i in range(size)]
            if kind:
                own.append(totals.pop())
            sent += [total.astype(BF16) for total in totals]
        parts.append([swapped(block, "chan", mask) for block, mask in zip(sent, even)])
    grad_blocks = []
    for which in range(2):
        grad_gated = own[which]
        for part in parts[which]:
            grad_gated = grad_gated + part.astype(F32)
        gate_part = gate[which * SUB : (which + 1) * SUB].astype(F32)
        grad_conv = (gate_part * grad_gated).astype(BF16)
        gate, grad_conv = lax.optimization_barrier((gate, grad_conv))
        grad_blocks.append(spread_blocks(grad_conv, "seq"))
    seq_n = lax.axis_size("seq")
    groups_of = stages(seq_n)
    total = None
    for i, (which, offsets) in enumerate(groups_of):
        last = i == len(groups_of) - 1
        chosen = {offset: grad_blocks[which][offset] for offset in offsets}
        total = add_blocks(seq_n, dft, lags, chosen, which, total, back if last else None)
    return tuple(total)


def stages(seq_n):
    near = [0, 1] if seq_n > 1 else [0]
    rest = [offset for offset in range(seq_n) if offset not in near]
    return [(0, list(range(seq_n))), (1, near)] + ([(1, rest)] if rest else [])


def solution(mesh):
    placed = (
        P("seq", "chan"),
        P("chan", None),
        P("seq", "chan"),
        P("seq", "chan"),
        P("seq", "chan"),
    )

    return jax.shard_map(
        body,
        mesh=mesh,
        in_specs=placed,
        out_specs=(P("seq", "chan"), P("seq", "chan")),
        check_vma=False,
    )
```
